128 devices in a mesh: node: 16 (over y, z), local: 8 (over x, core).
Axes of the slice: x: 4, y: 4, z: 4, core: 2. Of those that a mesh axis runs over, the one named last changes fastest.
Arguments:
- tokens: bfloat16 [8192, 3584], P(('node', 'local')), may hold values from -6 to 6
- expert_ids: int32 [8192, 8], P(('node', 'local')), may hold values from 0 to 63, all different within a row; in each aligned block of 64 rows (0 to 63, 64 to 127, ...) at most 12 rows name the same one
- gate_values: float32 [8192, 8], P(('node', 'local')), may hold values from 0.1 to 1
- holder: int32 [64], replicated, may hold values from 0 to 63, each once
- matching: int32 [16], replicated, may hold values from 0 to 15, as said below
- gate_weight: bfloat16 [128, 3584, 512], P(('node', 'local')), may hold values from -0.09375 to 0.09375
- up_weight: bfloat16 [128, 3584, 512], P(('node', 'local')), may hold values from -0.09375 to 0.09375
- down_weight: bfloat16 [128, 512, 3584], P(('node', 'local')), may hold values from -0.1875 to 0.1875
Outputs:
- moe_out: bfloat16 [8192, 3584], P(('node', 'local'))
- new_gate: bfloat16 [128, 3584, 512], P(('node', 'local'))
- new_up: bfloat16 [128, 3584, 512], P(('node', 'local'))
- new_down: bfloat16 [128, 512, 3584], P(('node', 'local'))
The draws below stay inside these ranges and needn't reach their ends.
Inputs may be any that keep to these rules, and one draw needn't show every extreme that they name: `expert_ids`: each row names 8 different experts. In the 64 rows of one device no expert is named more than 12 times, and some device names some expert exactly 12 times. `holder`: each expert appears once. A perfect matching of the nodes: matching[matching[n]] == n and matching[n] != n.
All inputs are finite; a program needn't handle non-finite values.
Results may differ from the reference program's by a relative error of at most 0.0065.
Values may be sent and summed in bfloat16 or wider, within the bound.
No kernel may reach another device: no remote copies, remote signals or barrier semaphores. Data moves between devices by JAX's collectives and lax.ppermute only.
A program may use at most 192 MiB of HBM per device.

```python
import math
import jax
import jax.numpy as jnp
import numpy as np
from jax import lax

D = 3584
FF = 1024
TOP = 8
TOK_DEV = 64
EXPERTS = 64
CAP = 12
TOKENS = 8192
N_NODE = 16
N_LOCAL = 8


def draw_matching(key, part):
    shuffled = jax.random.permutation(key, N_NODE).astype(jnp.int32)
    couples = shuffled.reshape(N_NODE // 2, 2)
    partner = jnp.zeros((N_NODE,), jnp.int32)
    partner = partner.at[couples[:, 0]].set(couples[:, 1])
    partner = partner.at[couples[:, 1]].set(couples[:, 0])
    return partner


def block_scale(own_key, dims, shards, least, largest):
    def one(position, parts):
        draws = jax.random.uniform(jax.random.fold_in(jax.random.fold_in(own_key, 6), position), (parts,), jnp.float32, least / len(shards), largest / len(shards))
        return jnp.repeat(jnp.exp(draws), dims[position] // parts).reshape((-1,) + (1,) * (len(dims) - position - 1))

    loudness = one(*shards[0])
    for cut in shards[1:]:
        loudness = loudness * one(*cut)
    return loudness


def shared_out(own_key, own, number, rows, number_of, top, most, slope):
    ranking = jax.random.permutation(own_key, number_of)
    packed, usual = load_shares(number_of, rows * top, most, slope, True), load_shares(number_of, rows * top, most, slope, False)
    places = jnp.arange(number_of)

    def named(lengths, turn):
        used = int((lengths > 0).sum())
        fixed = max(1, used // 4)
        moved = fixed + (places - fixed + turn * (used - fixed)) % max(1, number_of - fixed)
        return jnp.zeros((number_of,), jnp.int32).at[ranking[jnp.where(places < fixed, places, moved)]].set(jnp.asarray(lengths, jnp.int32))

    lengths = jnp.where(number % 4 == 0, named(packed, number // 4), named(usual, number - number // 4 - 1))
    mixed = jax.random.permutation(jax.random.fold_in(own, 3), number_of)
    source_of, taker = mixed[0:number_of // 2 * 2:2], mixed[1:number_of // 2 * 2:2]
    margin = jnp.minimum(lengths[source_of] - 1, most - lengths[taker]) // 2
    margin = jnp.where((source_of == ranking[0]) | (taker == ranking[0]) | (lengths[taker] == 0), 0, jnp.maximum(margin, 0))
    moved = jax.random.randint(jax.random.fold_in(own, 4), (number_of // 2,), 0, 1 << 20) % (margin + 1)
    lengths = lengths.at[source_of].add(-moved).at[taker].add(moved)
    labels = jnp.searchsorted(jnp.cumsum(lengths), jnp.arange(rows * top), side="right").astype(jnp.int32)
    table = labels.reshape(top, rows).T
    table = table[jax.random.permutation(jax.random.fold_in(own, 1), rows)]
    turn = jax.random.randint(jax.random.fold_in(own, 2), (rows, 1), 0, top)
    return jnp.take_along_axis(table, (jnp.arange(top)[None, :] + turn) % top, axis=1)


def load_shares(amount, total, bound, lean, full):
    portions = [(1 << 20) // math.isqrt(rank ** lean) + 1 for rank in range(1, amount + 1)]
    largest = bound if full else min(bound, max(-(-total // amount), total * portions[0] // sum(portions)))
    least = 1 if total - largest >= amount - 1 else 0
    holding, surplus = [largest] + [least] * (amount - 1), total - largest - least * (amount - 1)
    while surplus > 0:
        candidates = [i for i in range(1, amount) if holding[i] < largest] or [i for i in range(1, amount) if holding[i] < bound]
        mass, budget = sum([portions[i] for i in candidates]), surplus
        for i in candidates:
            extra = min(bound - holding[i], max(1, budget * portions[i] // mass), surplus)
            holding[i] = holding[i] + extra
            surplus = surplus - extra
    return np.array(holding)


def centred(rng, shape, deviation, limit, cuts=(), kind=jnp.bfloat16):
    values = deviation * jax.random.normal(rng, shape, jnp.float32)
    if cuts:
        values = values * block_scale(rng, shape, cuts, -0.22, 0.18)
    return jnp.clip(values, -limit, limit).astype(kind)


def setup_inputs(seed: int = 0) -> dict:
    seeds = jax.random.split(jax.random.key(seed), 9)
    tokens = centred(seeds[0], (TOKENS, D), 1.0, 6.0, ((0, 128),))
    expert_ids_keys = jax.random.split(jax.random.fold_in(seeds[1], 1), TOKENS // TOK_DEV)
    expert_ids_turns = jax.random.permutation(jax.random.fold_in(seeds[1], 3), TOKENS // TOK_DEV)
    expert_ids = jax.vmap(lambda own, number: shared_out(jax.random.fold_in(seeds[1], 2), own, number, TOK_DEV, EXPERTS, TOP, CAP, 2))(expert_ids_keys, expert_ids_turns).reshape((TOKENS, TOP))
    gate_values = jnp.clip(0.1 + 0.9 * jax.random.uniform(seeds[2], (TOKENS, TOP), jnp.float32) ** block_scale(seeds[2], (TOKENS, TOP), ((0, 128),), -0.2, 0.2), 0.1, 1.0)
    holder = jax.random.permutation(seeds[3], EXPERTS).astype(jnp.int32)
    matching = draw_matching(jax.random.fold_in(seeds[8], 71), 0)
    gate_weight = centred(seeds[5], (2 * EXPERTS, D, FF // 2), D ** -0.5, 0.09375, ((0, 128),))
    up_weight = centred(seeds[6], (2 * EXPERTS, D, FF // 2), D ** -0.5, 0.09375, ((0, 128),))
    down_weight = centred(seeds[7], (2 * EXPERTS, FF // 2, D), FF ** -0.5, 0.1875, ((0, 128),))
    return dict(tokens=tokens, expert_ids=expert_ids, gate_values=gate_values, holder=holder, matching=matching, gate_weight=gate_weight, up_weight=up_weight, down_weight=down_weight)


def reference(tokens, expert_ids, gate_values, holder, matching, gate_weight, up_weight, down_weight):
    row_limit = N_NODE * N_LOCAL * CAP
    expert_range = jnp.arange(EXPERTS, dtype=jnp.int32)
    slot_of_expert = jnp.zeros((EXPERTS,), jnp.int32).at[holder].set(expert_range)
    flat_expert = expert_ids.reshape(-1)
    flat_gate = gate_values.reshape(-1)
    sorted_routes = jnp.argsort(flat_expert, stable=True).astype(jnp.int32)
    counts = jnp.sum((flat_expert[:, None] == expert_range[None, :]).astype(jnp.int32), axis=0)
    starts = (jnp.cumsum(counts) - counts).astype(jnp.int32)
    padded_order = jnp.concatenate([sorted_routes, jnp.zeros((row_limit,), jnp.int32)])
    running = jnp.zeros((TOKENS, D), jnp.float32)

    def accumulate(running, expert):
        picked = lax.dynamic_slice(padded_order, (starts[expert],), (row_limit,))
        is_live = jnp.arange(row_limit) < counts[expert]
        token_index = (picked // TOP).astype(jnp.int32)
        row_block = tokens[token_index]
        slot_here = slot_of_expert[expert]
        result = jnp.zeros((row_limit, D), jnp.float32)
        for part_index in range(2):
            row_index = 2 * slot_here + part_index
            gate_proj = jnp.dot(row_block, gate_weight[row_index], preferred_element_type=jnp.float32)
            up_proj = jnp.dot(row_block, up_weight[row_index], preferred_element_type=jnp.float32)
            hidden = (jax.nn.silu(gate_proj) * up_proj).astype(jnp.bfloat16)
            partial_value = jnp.dot(hidden, down_weight[row_index], preferred_element_type=jnp.float32).astype(jnp.bfloat16)
            result = result + partial_value.astype(jnp.float32)
        output = result.astype(jnp.bfloat16).astype(jnp.float32)
        weight = jnp.where(is_live, flat_gate[picked], 0.0)
        running = running.at[token_index].add(weight[:, None] * output)
        return running, None

    running, ignored = lax.scan(accumulate, running, expert_range)
    combined = running.astype(jnp.bfloat16)

    def reorder(matrix):
        grouped = matrix.reshape((N_NODE, matrix.shape[0] // N_NODE) + matrix.shape[1:])
        return grouped[matching].reshape(matrix.shape)

    return combined, reorder(gate_weight), reorder(up_weight), reorder(down_weight)
```

```python
import jax
import jax.numpy as jnp
from jax import lax
from jax.sharding import PartitionSpec as P

CAP_NUM, CAP_DEN = 3, 2
BF = jnp.bfloat16
F32 = jnp.float32


def along_x(block, hops, chips):
    pairs = [
        (2 * x + core, 2 * ((x + hops) % chips) + core) for x in range(chips) for core in range(2)
    ]
    return lax.ppermute(block, "local", pairs)


def other_core(block):
    size = lax.axis_size("local")
    return lax.ppermute(block, "local", [(i, i ^ 1) for i in range(size)])


def split_parts(matrix, pieces):
    return matrix.reshape((pieces, matrix.shape[1] // pieces, matrix.shape[2]))


def swap_weight(part, matching):
    nodes = lax.axis_size("node")
    arrived = lax.all_to_all(split_parts(part, nodes), "node", split_axis=0, concat_axis=0, tiled=True)
    reordered = jnp.take(arrived, matching, axis=0, mode="clip")
    returned = lax.all_to_all(reordered, "node", split_axis=0, concat_axis=0, tiled=True)
    return returned.reshape(part.shape)


def half_expert(rows, gate_part, up_part, down_part):
    gate_proj = jnp.dot(rows, gate_part, preferred_element_type=F32)
    up_proj = jnp.dot(rows, up_part, preferred_element_type=F32)
    hidden = (jax.nn.silu(gate_proj) * up_proj).astype(BF)
    return jnp.dot(hidden, down_part, preferred_element_type=F32).astype(BF)


def per_device(
    tokens, expert_ids, gate_values, holder, matching, gate_weight, up_weight, down_weight
):
    experts = holder.shape[0]
    tok_count, top_count = expert_ids.shape
    capacity = max(2, tok_count * top_count * CAP_NUM // (CAP_DEN * experts))
    feature_count = tokens.shape[1]
    nodes = lax.axis_size("node")
    chips = lax.axis_size("local") // 2
    my_node = lax.axis_index("node")
    my_chip = lax.axis_index("local") // 2
    weights = (gate_weight, up_weight, down_weight)

    pad = jnp.zeros((tok_count, 128 - 2 * top_count), BF)
    sent = jnp.concatenate(
        [tokens, expert_ids.astype(BF), gate_values.astype(BF), pad], axis=1
    )
    gathered = lax.all_gather(sent, "node", axis=0, tiled=True)
    total = nodes * tok_count
    token_rows = gathered[:, :feature_count]
    ids = gathered[:, feature_count : feature_count + top_count].astype(jnp.int32)
    gates = gathered[:, feature_count + top_count : feature_count + 2 * top_count].astype(F32)

    chip_order = (my_chip + jnp.arange(chips)) % chips
    here = holder[my_node * chips + chip_order]
    match = ids[:, :, None] == here[None, None, :]
    routed = jnp.any(match, axis=1)
    gate_of = jnp.sum(jnp.where(match, gates[:, :, None], 0.0), axis=1)
    before = (jnp.arange(tok_count)[:, None] > jnp.arange(tok_count)[None, :]).astype(BF)
    position = jnp.einsum(
        "ij,sjx->six",
        before,
        routed.astype(BF).reshape(nodes, tok_count, chips),
        preferred_element_type=F32,
    ).reshape(total, chips)
    source = (jnp.arange(total) // tok_count)[:, None]
    key = jnp.where(routed, source * capacity + position.astype(jnp.int32), -1)
    slots = nodes * capacity
    slot_range = jnp.arange(slots)

    blocks = []
    for hops in range(chips):
        pick = (slot_range[:, None] == key[None, :, hops]).astype(BF)
        blocks.append(jnp.dot(pick, token_rows, preferred_element_type=F32).astype(BF))
    rows = jnp.concatenate(
        [blocks[0]] + [along_x(blocks[hops], hops, chips) for hops in range(1, chips)], axis=0
    )
    mine = [w[0] for w in weights]
    others = [other_core(w) for w in mine]
    value = (half_expert(rows, *mine).astype(F32) + half_expert(rows, *others).astype(F32)).astype(BF)
    back = [value[:slots]] + [
        along_x(value[hops * slots : (hops + 1) * slots], -hops, chips) for hops in range(1, chips)
    ]
    weighted = jnp.concatenate(
        [
            jnp.where(key[:, hops, None] == slot_range[None, :], gate_of[:, hops, None], 0.0).astype(BF)
            for hops in range(chips)
        ],
        axis=1,
    )
    partial = jnp.dot(weighted, jnp.concatenate(back, axis=0), preferred_element_type=F32).astype(BF)
    combined = lax.psum_scatter(partial, "node", scatter_dimension=0, tiled=True)
    swapped = [swap_weight(w, matching) for w in weights]
    return (combined, *swapped)


def solution(mesh):
    both = ("node", "local")
    in_specs = (
        P(both, None),
        P(both, None),
        P(both, None),
        P(),
        P(),
        P(both, None, None),
        P(both, None, None),
        P(both, None, None),
    )
    out_specs = (P(both, None), P(both, None, None), P(both, None, None), P(both, None, None))
    return jax.shard_map(
        per_device, mesh=mesh, in_specs=in_specs, out_specs=out_specs, check_vma=False
    )
```

```python
import jax
import jax.numpy as jnp
from jax import lax
from jax.sharding import PartitionSpec as P


CAP_NUM, CAP_DEN = 3, 2
BF = jnp.bfloat16
F32 = jnp.float32


HOPS = (0, -1, 1, 2)


def along_x(block, hops, chips):
    pairs = [
        (2 * x + core, 2 * ((x + hops) % chips) + core) for x in range(chips) for core in range(2)
    ]
    return lax.ppermute(block, "local", pairs)


def along_node(block, axis, hops):
    side = 4
    if axis == "y":
        pairs = [(y * side + z, ((y + hops) % side) * side + z) for y in range(side) for z in range(side)]
    else:
        pairs = [(y * side + z, y * side + (z + hops) % side) for y in range(side) for z in range(side)]
    return lax.ppermute(block, "node", pairs)


def from_ring(block, axis):
    return [block] + [along_node(block, axis, -hops) for hops in HOPS[1:]]


def scatter_ring(blocks, axis):
    parts = [blocks[0]] + [along_node(blocks[i], axis, HOPS[i]) for i in (1, 2, 3)]
    return sum(p.astype(F32) for p in parts).astype(BF)


def other_core(block):
    size = lax.axis_size("local")
    return lax.ppermute(block, "local", [(i, i ^ 1) for i in range(size)])


def split_parts(matrix, pieces):
    return matrix.reshape((pieces, matrix.shape[1] // pieces, matrix.shape[2]))


def swap_weight(part, matching):
    nodes = lax.axis_size("node")
    arrived = lax.all_to_all(split_parts(part, nodes), "node", split_axis=0, concat_axis=0, tiled=True)
    reordered = jnp.take(arrived, matching, axis=0, mode="clip")
    returned = lax.all_to_all(reordered, "node", split_axis=0, concat_axis=0, tiled=True)
    return returned.reshape(part.shape)


def half_expert(rows, gate_part, up_part, down_part):
    gate_proj = jnp.dot(rows, gate_part, preferred_element_type=F32)
    up_proj = jnp.dot(rows, up_part, preferred_element_type=F32)
    hidden = (jax.nn.silu(gate_proj) * up_proj).astype(BF)
    return jnp.dot(hidden, down_part, preferred_element_type=F32).astype(BF)


def layer(
    tokens, expert_ids, gate_values, holder, matching, gate_weight, up_weight, down_weight
):
    experts = holder.shape[0]
    tok_count, top_count = expert_ids.shape
    capacity = max(2, tok_count * top_count * CAP_NUM // (CAP_DEN * experts))
    feature_count = tokens.shape[1]
    nodes = lax.axis_size("node")
    chips = lax.axis_size("local") // 2
    my_node = lax.axis_index("node")
    my_chip = lax.axis_index("local") // 2
    weights = (gate_weight, up_weight, down_weight)

    pad = jnp.zeros((tok_count, 128 - 2 * top_count), BF)
    sent = jnp.concatenate(
        [tokens, expert_ids.astype(BF), gate_values.astype(BF), pad], axis=1
    )
    half = tok_count // 2
    first = jnp.concatenate(from_ring(sent[:half], "y"), axis=0)
    second = jnp.concatenate(from_ring(sent[half:], "z"), axis=0)
    first, second = lax.optimization_barrier((first, second))
    pieces = from_ring(first, "z") + from_ring(second, "y")
    total = nodes * tok_count
    gathered = jnp.concatenate(pieces, axis=0)
    token_rows = gathered[:, :feature_count]

    def in_order(columns):
        one = columns[: total // 2].reshape(4, 4, half, -1)
        two = columns[total // 2 :].reshape(4, 4, half, -1).transpose(1, 0, 2, 3)
        return jnp.concatenate([one, two], axis=2).reshape(total, -1)

    def as_rows(columns):
        both = columns.reshape(4, 4, 2, half, -1)
        one = both[:, :, 0].reshape(total // 2, -1)
        two = both[:, :, 1].transpose(1, 0, 2, 3).reshape(total // 2, -1)
        return jnp.concatenate([one, two], axis=0)

    routes = in_order(gathered[:, feature_count : feature_count + 2 * top_count])
    ids = routes[:, :top_count].astype(jnp.int32)
    gates = routes[:, top_count:].astype(F32)

    chip_order = (my_chip + jnp.arange(chips)) % chips
    here = holder[my_node * chips + chip_order]
    match = ids[:, :, None] == here[None, None, :]
    routed = jnp.any(match, axis=1)
    gate_of = jnp.sum(jnp.where(match, gates[:, :, None], 0.0), axis=1)
    before = (jnp.arange(tok_count)[:, None] > jnp.arange(tok_count)[None, :]).astype(BF)
    position = jnp.einsum(
        "ij,sjx->six",
        before,
        routed.astype(BF).reshape(nodes, tok_count, chips),
        preferred_element_type=F32,
    ).reshape(total, chips)
    source = (jnp.arange(total) // tok_count)[:, None]
    key = jnp.where(routed, source * capacity + position.astype(jnp.int32), -1)
    key = as_rows(key)
    gate_of = as_rows(gate_of)
    slots = nodes * capacity
    slot_range = jnp.arange(slots)

    blocks = []
    for hops in range(chips):
        pick = (slot_range[:, None] == key[None, :, hops]).astype(BF)
        blocks.append(jnp.dot(pick, token_rows, preferred_element_type=F32).astype(BF))
    rows = [blocks[0]] + [along_x(blocks[hops], hops, chips) for hops in range(1, chips)]
    rows = jnp.concatenate(rows, axis=0)
    mine = [w[0] for w in weights]
    others = [other_core(w) for w in mine]
    own = half_expert(rows, *mine)
    value = (own.astype(F32) + half_expert(rows, *others).astype(F32)).astype(BF)
    back = [value[:slots]] + [
        along_x(value[hops * slots : (hops + 1) * slots], -hops, chips) for hops in range(1, chips)
    ]
    weighted = [
        jnp.where(key[:, hops, None] == slot_range[None, :], gate_of[:, hops, None], 0.0).astype(BF)
        for hops in range(chips)
    ]
    partial = jnp.dot(
        jnp.concatenate(weighted, axis=1), jnp.concatenate(back, axis=0), preferred_element_type=F32
    ).astype(BF)
    one = partial[: total // 2].reshape(4, 4 * half, feature_count)
    two = partial[total // 2 :].reshape(4, 4 * half, feature_count)
    one = scatter_ring([one[i] for i in range(4)], "z").reshape(4, half, feature_count)
    two = scatter_ring([two[i] for i in range(4)], "y").reshape(4, half, feature_count)
    one, two = lax.optimization_barrier((one, two))
    one = scatter_ring([one[i] for i in range(4)], "y")
    two = scatter_ring([two[i] for i in range(4)], "z")
    combined = jnp.concatenate([one, two], axis=0)
    swapped = [swap_weight(w, matching) for w in weights]
    return (combined, *swapped)


def solution(mesh):
    both = ("node", "local")
    in_specs = (
        P(both, None),
        P(both, None),
        P(both, None),
        P(),
        P(),
        P(both, None, None),
        P(both, None, None),
        P(both, None, None),
    )
    out_specs = (P(both, None), P(both, None, None), P(both, None, None), P(both, None, None))
    return jax.shard_map(layer, mesh=mesh, in_specs=in_specs, out_specs=out_specs, check_vma=False)
```

```python
import jax
import jax.numpy as jnp
from jax import lax
from jax.experimental import pallas as pl
from jax.sharding import PartitionSpec as P


CAP_NUM, CAP_DEN = 3, 2
BF = jnp.bfloat16
F32 = jnp.float32


HOPS = (0, -1, 1, 2)


def along_x(block, hops, chips):
    pairs = [
        (2 * x + core, 2 * ((x + hops) % chips) + core) for x in range(chips) for core in range(2)
    ]
    return lax.ppermute(block, "local", pairs)


def along_node(block, axis, hops):
    side = 4
    if axis == "y":
        pairs = [(y * side + z, ((y + hops) % side) * side + z) for y in range(side) for z in range(side)]
    else:
        pairs = [(y * side + z, y * side + (z + hops) % side) for y in range(side) for z in range(side)]
    return lax.ppermute(block, "node", pairs)


def from_ring(block, axis):
    return [block] + [along_node(block, axis, -hops) for hops in HOPS[1:]]


def scatter_ring(blocks, axis):
    parts = [blocks[0]] + [along_node(blocks[i], axis, HOPS[i]) for i in (1, 2, 3)]
    return sum(p.astype(F32) for p in parts).astype(BF)


def other_core(block):
    size = lax.axis_size("local")
    return lax.ppermute(block, "local", [(i, i ^ 1) for i in range(size)])


def split_parts(matrix, pieces):
    return matrix.reshape((pieces, matrix.shape[1] // pieces, matrix.shape[2]))


def swap_weight(part, matching, name):
    nodes = lax.axis_size("node")
    arrived = lax.all_to_all(split_parts(part, nodes), "node", split_axis=0, concat_axis=0, tiled=True)
    reordered = jnp.take(arrived, matching, axis=0, mode="clip")
    returned = lax.all_to_all(reordered, "node", split_axis=0, concat_axis=0, tiled=True)
    if name == "d":
        return returned.reshape(part.shape)
    return keep(returned.reshape(part.shape[1:]), 4).reshape(part.shape)


def copy_kernel(in_ref, out_ref):
    out_ref[...] = in_ref[...]


def keep(matrix, steps):
    rows, columns = matrix.shape
    spec = pl.BlockSpec((rows // steps, columns), lambda i: (i, 0))
    return pl.pallas_call(
        copy_kernel,
        out_shape=jax.ShapeDtypeStruct(matrix.shape, matrix.dtype),
        grid=(steps,),
        in_specs=[spec],
        out_specs=spec,
        cost_estimate=pl.CostEstimate(flops=0, bytes_accessed=4 * rows * columns, transcendentals=0),
    )(matrix)


def half_expert(rows, gate_part, up_part, down_part):
    gate_proj = jnp.dot(rows, gate_part, preferred_element_type=F32)
    up_proj = jnp.dot(rows, up_part, preferred_element_type=F32)
    hidden = (jax.nn.silu(gate_proj) * up_proj).astype(BF)
    return jnp.dot(hidden, down_part, preferred_element_type=F32).astype(BF)


def layer(
    tokens, expert_ids, gate_values, holder, matching, gate_weight, up_weight, down_weight
):
    experts = holder.shape[0]
    tok_count, top_count = expert_ids.shape
    capacity = max(2, tok_count * top_count * CAP_NUM // (CAP_DEN * experts))
    feature_count = tokens.shape[1]
    nodes = lax.axis_size("node")
    chips = lax.axis_size("local") // 2
    my_node = lax.axis_index("node")
    my_chip = lax.axis_index("local") // 2
    weights = (gate_weight, up_weight, down_weight)

    pad = jnp.zeros((tok_count, 128 - 2 * top_count), BF)
    sent = jnp.concatenate(
        [tokens, expert_ids.astype(BF), gate_values.astype(BF), pad], axis=1
    )
    half = tok_count // 2
    first = jnp.concatenate(from_ring(sent[:half], "y"), axis=0)
    second = jnp.concatenate(from_ring(sent[half:], "z"), axis=0)
    first, second = lax.optimization_barrier((first, second))
    pieces = from_ring(first, "z") + from_ring(second, "y")
    total = nodes * tok_count
    gathered = jnp.concatenate(pieces, axis=0)
    token_rows = gathered[:, :feature_count]

    def in_order(columns):
        one = columns[: total // 2].reshape(4, 4, half, -1)
        two = columns[total // 2 :].reshape(4, 4, half, -1).transpose(1, 0, 2, 3)
        return jnp.concatenate([one, two], axis=2).reshape(total, -1)

    def as_rows(columns):
        both = columns.reshape(4, 4, 2, half, -1)
        one = both[:, :, 0].reshape(total // 2, -1)
        two = both[:, :, 1].transpose(1, 0, 2, 3).reshape(total // 2, -1)
        return jnp.concatenate([one, two], axis=0)

    routes = in_order(gathered[:, feature_count : feature_count + 2 * top_count])
    ids = routes[:, :top_count].astype(jnp.int32)
    gates = routes[:, top_count:].astype(F32)

    chip_order = (my_chip + jnp.arange(chips)) % chips
    here = holder[my_node * chips + chip_order]
    match = ids[:, :, None] == here[None, None, :]
    routed = jnp.any(match, axis=1)
    gate_of = jnp.sum(jnp.where(match, gates[:, :, None], 0.0), axis=1)
    before = (jnp.arange(tok_count)[:, None] > jnp.arange(tok_count)[None, :]).astype(BF)
    position = jnp.einsum(
        "ij,sjx->six",
        before,
        routed.astype(BF).reshape(nodes, tok_count, chips),
        preferred_element_type=F32,
    ).reshape(total, chips)
    source = (jnp.arange(total) // tok_count)[:, None]
    key = jnp.where(routed, source * capacity + position.astype(jnp.int32), -1)
    key = as_rows(key)
    gate_of = as_rows(gate_of)
    slots = nodes * capacity
    slot_range = jnp.arange(slots)

    blocks = []
    for hops in range(chips):
        pick = (slot_range[:, None] == key[None, :, hops]).astype(BF)
        blocks.append(jnp.dot(pick, token_rows, preferred_element_type=F32).astype(BF))
    rows = [blocks[0]] + [along_x(blocks[hops], hops, chips) for hops in range(1, chips)]
    rows = jnp.concatenate(rows, axis=0)
    mine = [w[0] for w in weights]
    others = [other_core(w) for w in mine]
    own = half_expert(rows, *mine)
    value = (own.astype(F32) + half_expert(rows, *others).astype(F32)).astype(BF)
    back = [value[:slots]] + [
        along_x(value[hops * slots : (hops + 1) * slots], -hops, chips) for hops in range(1, chips)
    ]
    weighted = [
        jnp.where(key[:, hops, None] == slot_range[None, :], gate_of[:, hops, None], 0.0).astype(BF)
        for hops in range(chips)
    ]
    partial = jnp.dot(
        jnp.concatenate(weighted, axis=1), jnp.concatenate(back, axis=0), preferred_element_type=F32
    ).astype(BF)
    one = partial[: total // 2].reshape(4, 4 * half, feature_count)
    two = partial[total // 2 :].reshape(4, 4 * half, feature_count)
    one = scatter_ring([one[i] for i in range(4)], "z").reshape(4, half, feature_count)
    two = scatter_ring([two[i] for i in range(4)], "y").reshape(4, half, feature_count)
    one, two = lax.optimization_barrier((one, two))
    one = scatter_ring([one[i] for i in range(4)], "y")
    two = scatter_ring([two[i] for i in range(4)], "z")
    combined = jnp.concatenate([one, two], axis=0)
    swapped = [swap_weight(w, matching, name) for w, name in zip(weights, "gud")]
    return (combined, *swapped)


def solution(mesh):
    both = ("node", "local")
    in_specs = (
        P(both, None),
        P(both, None),
        P(both, None),
        P(),
        P(),
        P(both, None, None),
        P(both, None, None),
        P(both, None, None),
    )
    out_specs = (P(both, None), P(both, None, None), P(both, None, None), P(both, None, None))
    return jax.shard_map(layer, mesh=mesh, in_specs=in_specs, out_specs=out_specs, check_vma=False)
```

```python
import jax
import jax.numpy as jnp
from jax import lax
from jax.experimental import pallas as pl
from jax.experimental.pallas import tpu as pltpu
from jax.sharding import PartitionSpec as P


CAP_NUM, CAP_DEN = 3, 2
BF = jnp.bfloat16
F32 = jnp.float32


HOPS = (0, -1, 1, 2)


def along_x(block, hops, chips):
    pairs = [
        (2 * x + core, 2 * ((x + hops) % chips) + core) for x in range(chips) for core in range(2)
    ]
    return lax.ppermute(block, "local", pairs)


def along_node(block, axis, hops):
    side = 4
    if axis == "y":
        pairs = [(y * side + z, ((y + hops) % side) * side + z) for y in range(side) for z in range(side)]
    else:
        pairs = [(y * side + z, y * side + (z + hops) % side) for y in range(side) for z in range(side)]
    return lax.ppermute(block, "node", pairs)


def from_ring(block, axis):
    return [block] + [along_node(block, axis, -hops) for hops in HOPS[1:]]


def relayed(below, above, axis):
    half = below.shape[0] // 2
    return jnp.concatenate(
        [along_node(below[:half], axis, 1), along_node(above[half:], axis, -1)], axis=0
    )


def scatter_ring(blocks, axis):
    parts = [blocks[0]] + [along_node(blocks[i], axis, HOPS[i]) for i in (1, 2, 3)]
    return sum(p.astype(F32) for p in parts).astype(BF)


def other_core(block):
    size = lax.axis_size("local")
    return lax.ppermute(block, "local", [(i, i ^ 1) for i in range(size)])


def split_parts(matrix, pieces):
    return matrix.reshape((pieces, matrix.shape[1] // pieces, matrix.shape[2]))


def swap_weight(part, matching):
    nodes = lax.axis_size("node")
    arrived = lax.all_to_all(split_parts(part, nodes), "node", split_axis=0, concat_axis=0, tiled=True)
    reordered = jnp.take(arrived, matching, axis=0, mode="clip")
    returned = lax.all_to_all(reordered, "node", split_axis=0, concat_axis=0, tiled=True)
    return keep(returned.reshape(part.shape[1:]), 4).reshape(part.shape)


def copy_kernel(in_ref, out_ref):
    out_ref[...] = in_ref[...]


def keep(matrix, steps):
    rows, columns = matrix.shape
    spec = pl.BlockSpec((rows // steps, columns), lambda i: (i, 0))
    return pl.pallas_call(
        copy_kernel,
        out_shape=jax.ShapeDtypeStruct(matrix.shape, matrix.dtype),
        grid=(steps,),
        in_specs=[spec],
        out_specs=spec,
        cost_estimate=pl.CostEstimate(flops=0, bytes_accessed=4 * rows * columns, transcendentals=0),
    )(matrix)


def pick_kernel(key_ref, *refs):
    hops, total = key_ref.shape
    pieces, outs, pick = refs[: -hops - 1], refs[-hops - 1 : -1], refs[-1]
    slots = outs[0].shape[0]

    @pl.when(pl.program_id(0) == 0)
    def _():
        slot = lax.broadcasted_iota(jnp.int32, (slots, total), 0)
        for h in range(hops):
            pick[h * slots : (h + 1) * slots, :] = jnp.where(slot == key_ref[h : h + 1, :], 1.0, 0.0).astype(BF)

    rows = jnp.concatenate([p[...] for p in pieces], axis=0)
    picked = jnp.dot(pick[...], rows, preferred_element_type=F32)
    for h in range(hops):
        outs[h][...] = picked[h * slots : (h + 1) * slots].astype(BF)


def pick_rows(key, pieces, slots, columns, tile=512):
    hops, total = key.shape
    return pl.pallas_call(
        pick_kernel,
        out_shape=[jax.ShapeDtypeStruct((slots, columns), BF)] * hops,
        grid=(columns // tile,),
        in_specs=[pl.BlockSpec((hops, total), lambda i: (0, 0))]
        + [pl.BlockSpec((p.shape[0], tile), lambda i: (0, i)) for p in pieces],
        out_specs=[pl.BlockSpec((slots, tile), lambda i: (0, i))] * hops,
        scratch_shapes=[pltpu.VMEM((hops * slots, total), BF)],
        cost_estimate=pl.CostEstimate(
            flops=2 * hops * slots * total * columns,
            bytes_accessed=2 * columns * (total + hops * slots),
            transcendentals=0,
        ),
    )(key, *pieces)


def add_kernel(key_ref, gate_ref, *refs):
    total, hops = key_ref.shape
    blocks, outs, weigh = refs[:hops], refs[hops:-1], refs[-1]
    slots = blocks[0].shape[0]

    @pl.when(pl.program_id(0) == 0)
    def _():
        slot = lax.broadcasted_iota(jnp.int32, (total, slots), 1)
        for h in range(hops):
            weigh[h] = jnp.where(slot == key_ref[:, h : h + 1], gate_ref[:, h : h + 1], 0.0).astype(BF)

    added = jnp.dot(weigh[0], blocks[0][...], preferred_element_type=F32)
    for h in range(1, hops):
        added += jnp.dot(weigh[h], blocks[h][...], preferred_element_type=F32)
    rows = outs[0].shape[0]
    for r, out in enumerate(outs):
        out[...] = added[r * rows : (r + 1) * rows].astype(BF)


def add_rows(key, gate, blocks, parts, tile=512):
    total, hops = key.shape
    slots, columns = blocks[0].shape
    return pl.pallas_call(
        add_kernel,
        out_shape=[jax.ShapeDtypeStruct((total // parts, columns), BF)] * parts,
        grid=(columns // tile,),
        in_specs=[pl.BlockSpec((total, hops), lambda i: (0, 0))] * 2
        + [pl.BlockSpec((slots, tile), lambda i: (0, i))] * hops,
        out_specs=[pl.BlockSpec((total // parts, tile), lambda i: (0, i))] * parts,
        scratch_shapes=[pltpu.VMEM((hops, total, slots), BF)],
        cost_estimate=pl.CostEstimate(
            flops=2 * hops * slots * total * columns,
            bytes_accessed=2 * columns * (total + hops * slots),
            transcendentals=0,
        ),
    )(key, gate, *blocks)


def half_expert(rows, gate_part, up_part, down_part):
    gate_proj = jnp.dot(rows, gate_part, preferred_element_type=F32)
    up_proj = jnp.dot(rows, up_part, preferred_element_type=F32)
    hidden = (jax.nn.silu(gate_proj) * up_proj).astype(BF)
    return jnp.dot(hidden, down_part, preferred_element_type=F32).astype(BF)


def layer(
    tokens, expert_ids, gate_values, holder, matching, gate_weight, up_weight, down_weight
):
    experts = holder.shape[0]
    tok_count, top_count = expert_ids.shape
    capacity = max(2, tok_count * top_count * CAP_NUM // (CAP_DEN * experts))
    feature_count = tokens.shape[1]
    nodes = lax.axis_size("node")
    chips = lax.axis_size("local") // 2
    my_node = lax.axis_index("node")
    my_chip = lax.axis_index("local") // 2
    weights = (gate_weight, up_weight, down_weight)

    pad = jnp.zeros((tok_count, 128 - 2 * top_count), BF)
    sent = jnp.concatenate(
        [tokens, expert_ids.astype(BF), gate_values.astype(BF), pad], axis=1
    )
    half = tok_count // 2
    first = jnp.concatenate(from_ring(sent[:half], "y"), axis=0)
    second = jnp.concatenate(from_ring(sent[half:], "z"), axis=0)
    first, second = lax.optimization_barrier((first, second))
    lower, upper = along_node(first, "z", 1), along_node(first, "z", -1)
    left, right = along_node(second, "y", 1), along_node(second, "y", -1)
    pieces = [first, lower, upper, relayed(lower, upper, "z")]
    pieces += [second, left, right, relayed(left, right, "y")]
    total = nodes * tok_count
    routes = jnp.concatenate(
        [p[:, feature_count : feature_count + 2 * top_count] for p in pieces], axis=0
    )
    ids = routes[:, :top_count].astype(jnp.int32)
    gates = routes[:, top_count:].astype(F32)

    chip_order = (my_chip + jnp.arange(chips)) % chips
    here = holder[my_node * chips + chip_order]
    match = ids[:, :, None] == here[None, None, :]
    routed = jnp.any(match, axis=1)
    gate_of = jnp.sum(jnp.where(match, gates[:, :, None], 0.0), axis=1)

    row = jnp.arange(total)
    turn, outer, inner = row // (total // 2), row // (4 * half) % 4, row // half % 4
    source = jnp.where(turn == 0, outer * 4 + inner, inner * 4 + outer)
    place = turn * half + row % half
    before = (source[:, None] == source[None, :]) & (place[:, None] > place[None, :])
    position = jnp.dot(before.astype(BF), routed.astype(BF), preferred_element_type=F32)
    key = jnp.where(routed, source[:, None] * capacity + position.astype(jnp.int32), -1)
    slots = nodes * capacity

    blocks = pick_rows(key.T, pieces, slots, feature_count)
    rows = [blocks[0]] + [along_x(blocks[hops], hops, chips) for hops in range(1, chips)]
    rows = jnp.concatenate(rows, axis=0)
    mine = [w[0] for w in weights]
    others = [other_core(w) for w in mine]
    own = half_expert(rows, *mine)
    value = (own.astype(F32) + half_expert(rows, *others).astype(F32)).astype(BF)
    back = [value[:slots]] + [
        along_x(value[hops * slots : (hops + 1) * slots], -hops, chips) for hops in range(1, chips)
    ]
    parts = add_rows(key, gate_of, back, 8)
    one = scatter_ring(parts[:4], "z").reshape(4, half, feature_count)
    two = scatter_ring(parts[4:], "y").reshape(4, half, feature_count)
    one, two = lax.optimization_barrier((one, two))
    one = scatter_ring([one[i] for i in range(4)], "y")
    two = scatter_ring([two[i] for i in range(4)], "z")
    combined = jnp.concatenate([one, two], axis=0)
    swapped = [swap_weight(w, matching) for w in weights]
    return (combined, *swapped)


def solution(mesh):
    both = ("node", "local")
    in_specs = (
        P(both, None),
        P(both, None),
        P(both, None),
        P(),
        P(),
        P(both, None, None),
        P(both, None, None),
        P(both, None, None),
    )
    out_specs = (P(both, None), P(both, None, None), P(both, None, None), P(both, None, None))
    return jax.shard_map(layer, mesh=mesh, in_specs=in_specs, out_specs=out_specs, check_vma=False)
```

```python
import jax
import jax.numpy as jnp
from jax import lax
from jax.experimental import pallas as pl
from jax.experimental.pallas import tpu as pltpu
from jax.sharding import PartitionSpec as P


CAP_NUM, CAP_DEN = 3, 2
BF = jnp.bfloat16
F32 = jnp.float32


HOPS = (0, -1, 1, 2)


def along_x(block, hops, chips):
    pairs = [
        (2 * x + core, 2 * ((x + hops) % chips) + core) for x in range(chips) for core in range(2)
    ]
    return lax.ppermute(block, "local", pairs)


def along_node(block, axis, hops):
    side = 4
    if axis == "y":
        pairs = [(y * side + z, ((y + hops) % side) * side + z) for y in range(side) for z in range(side)]
    else:
        pairs = [(y * side + z, y * side + (z + hops) % side) for y in range(side) for z in range(side)]
    return lax.ppermute(block, "node", pairs)


def from_ring(block, axis):
    return [block] + [along_node(block, axis, -hops) for hops in HOPS[1:]]


def relayed(below, above, axis):
    half = below.shape[0] // 2
    return jnp.concatenate(
        [along_node(below[:half], axis, 1), along_node(above[half:], axis, -1)], axis=0
    )


def scatter_ring(blocks, axis):
    parts = [blocks[0]] + [along_node(blocks[i], axis, HOPS[i]) for i in (1, 2, 3)]
    return sum(p.astype(F32) for p in parts).astype(BF)


def other_core(block):
    size = lax.axis_size("local")
    return lax.ppermute(block, "local", [(i, i ^ 1) for i in range(size)])


def split_parts(matrix, pieces):
    return matrix.reshape((pieces, matrix.shape[1] // pieces, matrix.shape[2]))


def swap_weight(part, matching):
    nodes = lax.axis_size("node")
    arrived = lax.all_to_all(split_parts(part, nodes), "node", split_axis=0, concat_axis=0, tiled=True)
    reordered = jnp.take(arrived, matching, axis=0, mode="clip")
    returned = lax.all_to_all(reordered, "node", split_axis=0, concat_axis=0, tiled=True)
    return keep(returned.reshape(part.shape[1:]), 4).reshape(part.shape)


def copy_kernel(in_ref, out_ref):
    out_ref[...] = in_ref[...]


def keep(matrix, steps):
    rows, columns = matrix.shape
    spec = pl.BlockSpec((rows // steps, columns), lambda i: (i, 0))
    return pl.pallas_call(
        copy_kernel,
        out_shape=jax.ShapeDtypeStruct(matrix.shape, matrix.dtype),
        grid=(steps,),
        in_specs=[spec],
        out_specs=spec,
        cost_estimate=pl.CostEstimate(flops=0, bytes_accessed=4 * rows * columns, transcendentals=0),
    )(matrix)


def pick_kernel(key_ref, *refs):
    hops, total = key_ref.shape
    pieces, outs, pick = refs[: -hops - 1], refs[-hops - 1 : -1], refs[-1]
    slots = outs[0].shape[0]

    @pl.when(pl.program_id(0) == 0)
    def _():
        slot = lax.broadcasted_iota(jnp.int32, (slots, total), 0)
        for h in range(hops):
            pick[h * slots : (h + 1) * slots, :] = jnp.where(slot == key_ref[h : h + 1, :], 1.0, 0.0).astype(BF)

    rows = jnp.concatenate([p[...] for p in pieces], axis=0)
    picked = jnp.dot(pick[...], rows, preferred_element_type=F32)
    for h in range(hops):
        outs[h][...] = picked[h * slots : (h + 1) * slots].astype(BF)


def pick_rows(key, pieces, slots, columns, tile=512):
    hops, total = key.shape
    return pl.pallas_call(
        pick_kernel,
        out_shape=[jax.ShapeDtypeStruct((slots, columns), BF)] * hops,
        grid=(columns // tile,),
        in_specs=[pl.BlockSpec((hops, total), lambda i: (0, 0))]
        + [pl.BlockSpec((p.shape[0], tile), lambda i: (0, i)) for p in pieces],
        out_specs=[pl.BlockSpec((slots, tile), lambda i: (0, i))] * hops,
        scratch_shapes=[pltpu.VMEM((hops * slots, total), BF)],
        cost_estimate=pl.CostEstimate(
            flops=2 * hops * slots * total * columns,
            bytes_accessed=2 * columns * (total + hops * slots),
            transcendentals=0,
        ),
    )(key, *pieces)


def add_kernel(key_ref, gate_ref, *refs):
    total, hops = key_ref.shape
    blocks, outs, weigh = refs[:hops], refs[hops:-1], refs[-1]
    slots = blocks[0].shape[0]

    @pl.when(pl.program_id(0) == 0)
    def _():
        slot = lax.broadcasted_iota(jnp.int32, (total, slots), 1)
        for h in range(hops):
            weigh[h] = jnp.where(slot == key_ref[:, h : h + 1], gate_ref[:, h : h + 1], 0.0).astype(BF)

    added = jnp.dot(weigh[0], blocks[0][...], preferred_element_type=F32)
    for h in range(1, hops):
        added += jnp.dot(weigh[h], blocks[h][...], preferred_element_type=F32)
    rows = outs[0].shape[0]
    for r, out in enumerate(outs):
        out[...] = added[r * rows : (r + 1) * rows].astype(BF)


def add_rows(key, gate, blocks, parts, tile=512):
    total, hops = key.shape
    slots, columns = blocks[0].shape
    return pl.pallas_call(
        add_kernel,
        out_shape=[jax.ShapeDtypeStruct((total // parts, columns), BF)] * parts,
        grid=(columns // tile,),
        in_specs=[pl.BlockSpec((total, hops), lambda i: (0, 0))] * 2
        + [pl.BlockSpec((slots, tile), lambda i: (0, i))] * hops,
        out_specs=[pl.BlockSpec((total // parts, tile), lambda i: (0, i))] * parts,
        scratch_shapes=[pltpu.VMEM((hops, total, slots), BF)],
        cost_estimate=pl.CostEstimate(
            flops=2 * hops * slots * total * columns,
            bytes_accessed=2 * columns * (total + hops * slots),
            transcendentals=0,
        ),
    )(key, gate, *blocks)


def half_expert(rows, gate_part, up_part, down_part):
    gate_proj = jnp.dot(rows, gate_part, preferred_element_type=F32)
    up_proj = jnp.dot(rows, up_part, preferred_element_type=F32)
    hidden = (jax.nn.silu(gate_proj) * up_proj).astype(BF)
    return jnp.dot(hidden, down_part, preferred_element_type=F32).astype(BF)


def layer(
    tokens, expert_ids, gate_values, holder, matching, gate_weight, up_weight, down_weight
):
    experts = holder.shape[0]
    tok_count, top_count = expert_ids.shape
    capacity = max(2, tok_count * top_count * CAP_NUM // (CAP_DEN * experts))
    feature_count = tokens.shape[1]
    nodes = lax.axis_size("node")
    chips = lax.axis_size("local") // 2
    my_node = lax.axis_index("node")
    my_chip = lax.axis_index("local") // 2
    weights = (gate_weight, up_weight, down_weight)

    pad = jnp.zeros((tok_count, 128 - 2 * top_count), BF)
    sent = jnp.concatenate(
        [tokens, expert_ids.astype(BF), gate_values.astype(BF), pad], axis=1
    )
    half = tok_count // 2
    first = jnp.concatenate(from_ring(sent[:half], "y"), axis=0)
    second = jnp.concatenate(from_ring(sent[half:], "z"), axis=0)
    first, second = lax.optimization_barrier((first, second))
    lower, upper = along_node(first, "z", 1), along_node(first, "z", -1)
    left, right = along_node(second, "y", 1), along_node(second, "y", -1)
    pieces = [first, lower, upper, relayed(lower, upper, "z")]
    pieces += [second, left, right, relayed(left, right, "y")]
    total = nodes * tok_count
    routes = jnp.concatenate(
        [p[:, feature_count : feature_count + 2 * top_count] for p in pieces], axis=0
    )
    ids = routes[:, :top_count].astype(jnp.int32)
    gates = routes[:, top_count:].astype(F32)

    chip_order = (my_chip + jnp.arange(chips)) % chips
    here = holder[my_node * chips + chip_order]
    match = ids[:, :, None] == here[None, None, :]
    routed = jnp.any(match, axis=1)
    gate_of = jnp.sum(jnp.where(match, gates[:, :, None], 0.0), axis=1)

    row = jnp.arange(total)
    turn, outer, inner = row // (total // 2), row // (4 * half) % 4, row // half % 4
    source = jnp.where(turn == 0, outer * 4 + inner, inner * 4 + outer)
    place = turn * half + row % half
    before = (source[:, None] == source[None, :]) & (place[:, None] > place[None, :])
    position = jnp.dot(before.astype(BF), routed.astype(BF), preferred_element_type=F32)
    key = jnp.where(routed, source[:, None] * capacity + position.astype(jnp.int32), -1)
    slots = nodes * capacity

    blocks = pick_rows(key.T, pieces, slots, feature_count)
    mine = [w[0] for w in weights]
    others = [other_core(w) for w in mine]

    def expert(rows):
        own = half_expert(rows, *mine)
        return (own.astype(F32) + half_expert(rows, *others).astype(F32)).astype(BF)

    right, left = along_x(blocks[1], 1, chips), along_x(blocks[3], 3, chips)
    across = along_x(blocks[2], 2, chips)
    value = expert(jnp.concatenate([right, left], axis=0))
    right, left = along_x(value[:slots], -1, chips), along_x(value[slots:], -3, chips)
    value = expert(jnp.concatenate([blocks[0], across], axis=0))
    across = along_x(value[slots:], -2, chips)
    back = [value[:slots], right, across, left]
    parts = add_rows(key, gate_of, back, 8)
    one = scatter_ring(parts[:4], "z").reshape(4, half, feature_count)
    two = scatter_ring(parts[4:], "y").reshape(4, half, feature_count)
    one, two = lax.optimization_barrier((one, two))
    one = scatter_ring([one[i] for i in range(4)], "y")
    two = scatter_ring([two[i] for i in range(4)], "z")
    combined = jnp.concatenate([one, two], axis=0)
    swapped = [swap_weight(w, matching) for w in weights]
    return (combined, *swapped)


def solution(mesh):
    both = ("node", "local")
    in_specs = (
        P(both, None),
        P(both, None),
        P(both, None),
        P(),
        P(),
        P(both, None, None),
        P(both, None, None),
        P(both, None, None),
    )
    out_specs = (P(both, None), P(both, None, None), P(both, None, None), P(both, None, None))
    return jax.shard_map(layer, mesh=mesh, in_specs=in_specs, out_specs=out_specs, check_vma=False)
```
